32 devices in a mesh: dp: 4 (over y, core), mp: 8 (over z, x).
Axes of the slice: x: 2, y: 2, z: 4, core: 2. Of those that a mesh axis runs over, the one named last changes fastest.
Arguments:
- query_rows: bfloat16 [8192, 16, 128], P('dp', 'mp'), may hold values from -8 to 8
- key_rows: bfloat16 [8192, 16, 128], P('dp', 'mp'), may hold values from -8 to 8
- value_rows: bfloat16 [8192, 16, 128], P('dp', 'mp'), may hold values from -6 to 6
- residual: bfloat16 [4096, 8, 768], P('dp', 'mp'), may hold values from -40 to 40
- lengths: int32 [64], replicated, may hold values from 1 to 256, as said below
- assignment: int32 [64], replicated, may hold values from 0 to 3, as said below
- out_proj: bfloat16 [1024, 1536], P(None, 'mp'), may hold values from -0.1875 to 0.1875
- norm_gain: float32 [1536], replicated, may hold values from 0.5 to 1.5
- norm_bias: float32 [1536], replicated, may hold values from -3 to 3
- glu_proj: bfloat16 [1536, 3072], P(None, 'mp'), may hold values from -0.15625 to 0.15625
- conv_taps: float32 [31, 1536], replicated, may hold values from -1 to 1
- batch_scale: float32 [1536], replicated, may hold values from 0.25 to 1.75
- batch_shift: float32 [1536], replicated, may hold values from -3 to 3
- down_proj: bfloat16 [1536, 1536], P(None, 'mp'), may hold values from -0.15625 to 0.15625
Outputs:
- encoded: bfloat16 [16384, 1536], P(('dp', 'mp'))
The draws below stay inside these ranges and needn't reach their ends.
Inputs may be any that keep to these rules, and one draw needn't show every extreme that they name: `lengths`: utterance u starts in data group u // 16; a data group holds its utterances in order of u from its first frame on, and its frames after them are padding. In every draw every data group sends exactly 256 frames in each of its 4 utterances to one and the same data group, so that this group receives 4 * 256 frames from every data group; the utterances one data group sends to one data group never have more frames together. `assignment`: every data group sends exactly 4 of its utterances to each data group, itself included. In its new group an utterance lies after those of lower number, from the first frame on, and the frames after them are padding.
All inputs are finite; a program needn't handle non-finite values.
Results may differ from the reference program's by a relative error of at most 0.0034.
Values may be sent and summed in bfloat16 or wider, within the bound.
A program may use at most 128 MiB of HBM per device.

```python
import math
import jax
import jax.numpy as jnp
from jax import lax

D = 1536
HEADS = 16
HD = 64
KERNEL = 31
HALF = 15
MAXLEN = 256
PIECES = 4
QBLK = 512
FEAT_DEV = 192
ROWS_G = 4096
ROWS = 16384
UTT_G = 16
UTTS = 64
N_DP = 4


def routing_tables(key):
    groups = UTTS // UTT_G
    routing_key = jax.random.fold_in(key, 7001)
    order_keys = jax.random.split(jax.random.fold_in(routing_key, 1), groups)
    orders = jax.vmap(lambda order_key: jax.random.permutation(order_key, UTT_G))(order_keys)
    targets = (orders // PIECES).reshape(UTTS).astype(jnp.int32)
    factor = jax.random.randint(jax.random.fold_in(routing_key, 2), (groups,), 1, 5)
    spread = jax.random.randint(jax.random.fold_in(routing_key, 3), (UTTS,), MAXLEN // 4, MAXLEN // 2 + 1)
    owner_group = jnp.arange(UTTS) // UTT_G
    spans_drawn = jnp.minimum(MAXLEN, factor[owner_group] * spread // 2)
    filled_group = jax.random.randint(jax.random.fold_in(routing_key, 4), (), 0, groups)
    heavy_group = (filled_group + 1) % groups
    spans_drawn = jnp.where(targets == heavy_group, MAXLEN - 1, spans_drawn)
    spans_drawn = jnp.where(targets == filled_group, MAXLEN, spans_drawn).astype(jnp.int32)
    return (spans_drawn, targets)


def draw_lengths(key, part):
    return routing_tables(key)[0]


def draw_assignment(key, part):
    return routing_tables(key)[1]


def pack_pairs(flat):
    return flat.reshape(ROWS // 2, 2, HEADS, HD).transpose(0, 2, 1, 3).reshape(ROWS // 2, HEADS, 2 * HD)


def drawn_pair(key):
    shape = (ROWS, HEADS * HD)
    query_key = jax.random.fold_in(key, 501)
    keys_key = jax.random.fold_in(key, 502)
    queries = jax.random.truncated_normal(query_key, -4.0, 4.0, shape, jnp.float32)
    keyset = jax.random.truncated_normal(keys_key, -4.0, 4.0, shape, jnp.float32)
    return (queries, keyset)


def draw_query_rows(key, part):
    return pack_pairs(drawn_pair(key)[0]).astype(jnp.bfloat16)


def draw_key_rows(key, part):
    return pack_pairs(drawn_pair(key)[1]).astype(jnp.bfloat16)


def draw_residual(key, part):
    row_scale = 0.3 * jnp.exp(jax.random.uniform(jax.random.fold_in(key, 601), (ROWS, 1), jnp.float32, 0.0, math.log(10.0)))
    column_scale = 0.3 * jnp.exp(jax.random.uniform(jax.random.fold_in(key, 602), (1, D), jnp.float32, 0.0, math.log(10.0)))
    basis = jax.random.truncated_normal(jax.random.fold_in(key, 605), -4.0, 4.0, (ROWS, D), jnp.float32)
    flat = basis * row_scale * column_scale
    blocks = D // FEAT_DEV
    packed = flat.reshape(ROWS // 4, 4, blocks, FEAT_DEV).transpose(0, 2, 1, 3).reshape(ROWS // 4, blocks, 4 * FEAT_DEV)
    return packed.astype(jnp.bfloat16)


def levels(rng, shape, shards, smallest, high):
    gain, own = 1.0, jax.random.fold_in(rng, 6)
    for dim, shards_of in shards:
        steps = jnp.exp(jax.random.uniform(jax.random.fold_in(own, dim), (shards_of,), jnp.float32, smallest / len(shards), high / len(shards)))
        gain = gain * jnp.repeat(steps, shape[dim] // shards_of).reshape([-1 if axis == dim else 1 for axis in range(len(shape))])
    return gain


def bell_draw(stream_key, extent, deviation, most, pieces=(), held_as=jnp.bfloat16):
    values = jax.random.normal(stream_key, extent, jnp.float32) * deviation
    if len(pieces) > 0:
        values = levels(stream_key, extent, pieces, -0.22, 0.18) * values
    return jnp.clip(values, min=-most, max=most).astype(held_as)


def setup_inputs(seed: int = 0) -> dict:
    seeds = jax.random.split(jax.random.key(seed), 15)
    query_rows = draw_query_rows(jax.random.fold_in(seeds[14], 71), 0)
    key_rows = draw_key_rows(jax.random.fold_in(seeds[14], 71), 0)
    value_rows = bell_draw(seeds[2], (ROWS // 2, HEADS, 2 * HD), 1.0, 6.0, ((0, 4), (1, 8)))
    residual = draw_residual(jax.random.fold_in(seeds[14], 71), 0)
    lengths = draw_lengths(jax.random.fold_in(seeds[14], 71), 0)
    assignment = draw_assignment(jax.random.fold_in(seeds[14], 71), 0)
    out_proj = bell_draw(seeds[6], (HEADS * HD, D), (HEADS * HD) ** -0.5, 0.1875, ((1, 8),))
    norm_gain = jnp.clip(1.0 + 0.1 * jax.random.normal(seeds[7], (D,), jnp.float32), 0.5, 1.5)
    norm_bias = bell_draw(seeds[8], (D,), 0.5, 3.0, (), jnp.float32)
    glu_proj = bell_draw(seeds[9], (D, 2 * D), D ** -0.5, 0.15625, ((1, 8),))
    conv_taps = bell_draw(seeds[10], (KERNEL, D), KERNEL ** -0.5, 1.0, (), jnp.float32)
    batch_scale = jnp.clip(1.0 + 0.15 * jax.random.normal(seeds[11], (D,), jnp.float32), 0.25, 1.75)
    batch_shift = bell_draw(seeds[12], (D,), 0.5, 3.0, (), jnp.float32)
    down_proj = bell_draw(seeds[13], (D, D), D ** -0.5, 0.15625, ((1, 8),))
    return dict(query_rows=query_rows, key_rows=key_rows, value_rows=value_rows, residual=residual, lengths=lengths, assignment=assignment, out_proj=out_proj, norm_gain=norm_gain, norm_bias=norm_bias, glu_proj=glu_proj, conv_taps=conv_taps, batch_scale=batch_scale, batch_shift=batch_shift, down_proj=down_proj)


EPS = 1e-05
MASKED = -1e+30

def unpack_pairs(packed):
    pair_rows, head_count, pair_width = packed.shape
    width = pair_width // 2
    return packed.reshape(pair_rows, head_count, 2, width).transpose(0, 2, 1, 3).reshape(pair_rows * 2, head_count * width)

def unpack_fours(packed):
    four_rows, block_count, four_width = packed.shape
    width = four_width // 4
    return packed.reshape(four_rows, block_count, 4, width).transpose(0, 2, 1, 3).reshape(four_rows * 4, block_count * width)

def utterance_tables(lengths, assignment):
    utterance = jnp.arange(UTTS, dtype=jnp.int32)
    source = utterance // UTT_G
    earlier = utterance[None, :] < utterance[:, None]
    same_source = source[None, :] == source[:, None]
    same_target = assignment[None, :] == assignment[:, None]
    span_table = jnp.broadcast_to(lengths[None, :], (UTTS, UTTS))
    nothing = jnp.zeros_like(span_table)
    before_start = lax.optimization_barrier(jnp.sum(jnp.where(earlier & same_source, span_table, nothing), axis=1))
    after_start = lax.optimization_barrier(jnp.sum(jnp.where(earlier & same_target, span_table, nothing), axis=1))
    return (source, before_start, after_start)

def find_frames(data_group, owner_group, first_frame, lengths, frames, lookup):
    position = jnp.arange(frames, dtype=jnp.int32)[:, None]
    matches = (owner_group[None, :] == data_group) & (position >= first_frame[None, :]) & (position < first_frame[None, :] + lengths[None, :])
    utterance = jnp.arange(lengths.shape[0], dtype=jnp.int32)[None, :]
    occupied_slots = jnp.any(matches, axis=1)
    segment = jnp.where(occupied_slots, lax.optimization_barrier(jnp.sum(jnp.where(matches, utterance, 0), axis=1)), -1).astype(jnp.int32)
    shifted = lax.optimization_barrier(jnp.sum(jnp.where(matches, lookup[None, :] - first_frame[None, :], 0), axis=1))
    source_row = jnp.where(occupied_slots, jnp.arange(frames, dtype=jnp.int32) + shifted, 0).astype(jnp.int32)
    return (segment, occupied_slots, source_row)

def attend(query_rows, key_rows, value_rows, segment):
    group_rows, width_per_head = query_rows.shape
    head_count = width_per_head // HD
    window = QBLK + 2 * MAXLEN
    score_scale = HD ** (-0.5)
    queries = query_rows.reshape(group_rows, head_count, HD).astype(jnp.float32)
    keyset = key_rows.reshape(group_rows, head_count, HD).astype(jnp.float32)
    valueset = value_rows.reshape(group_rows, head_count, HD).astype(jnp.float32)

    def attend_block(block_index, context):
        first_row = (block_index * QBLK).astype(jnp.int32)
        window_low = jnp.clip(first_row - MAXLEN, 0, group_rows - window).astype(jnp.int32)
        query_block = lax.dynamic_slice_in_dim(queries, first_row, QBLK, 0)
        key_block = lax.dynamic_slice_in_dim(keyset, window_low, window, 0)
        value_block = lax.dynamic_slice_in_dim(valueset, window_low, window, 0)
        segment_query = lax.dynamic_slice_in_dim(segment, first_row, QBLK, 0)
        segment_key = lax.dynamic_slice_in_dim(segment, window_low, window, 0)
        allowed = (segment_query[:, None] == segment_key[None, :]) & (segment_key[None, :] >= 0)
        scores = jnp.einsum('qhd,khd->hqk', query_block, key_block) * score_scale
        scores = jnp.where(allowed[None], scores, MASKED)
        highest = lax.optimization_barrier(jnp.max(scores, axis=2, keepdims=True))
        exponentials = jnp.exp(scores - highest)
        denominator = lax.optimization_barrier(jnp.sum(exponentials, axis=2, keepdims=True))
        weights = (exponentials / denominator).astype(jnp.bfloat16)
        blended = jnp.einsum('hqk,khd->qhd', weights.astype(jnp.float32), value_block)
        blended = jnp.where((segment_query >= 0)[:, None, None], blended, 0.0).astype(jnp.bfloat16)
        return lax.dynamic_update_slice_in_dim(context, blended.reshape(QBLK, width_per_head), first_row, 0)
    return lax.fori_loop(0, group_rows // QBLK, attend_block, jnp.zeros((group_rows, width_per_head), jnp.bfloat16))

def depthwise(gated_rows, segment, conv_taps):
    output_rows = gated_rows.shape[0] - 2 * HALF
    centre = segment[HALF:HALF + output_rows]
    accumulated = jnp.zeros((output_rows, gated_rows.shape[1]), jnp.float32)
    for tap_index in range(KERNEL):
        same_segment = (segment[tap_index:tap_index + output_rows] == centre)[:, None]
        term = jnp.where(same_segment, gated_rows[tap_index:tap_index + output_rows].astype(jnp.float32), 0.0)
        accumulated = accumulated + term * conv_taps[tap_index]
    return accumulated

def reference(query_rows, key_rows, value_rows, residual, lengths, assignment, out_proj, norm_gain, norm_bias, glu_proj, conv_taps, batch_scale, batch_shift, down_proj):
    query_flat = unpack_pairs(query_rows)
    key_flat = unpack_pairs(key_rows)
    value_flat = unpack_pairs(value_rows)
    residual_flat = unpack_fours(residual)
    source, before_start, after_start = utterance_tables(lengths, assignment)
    lookup = source * ROWS_G + before_start

    def one_group(data_group):
        segment, occupied_slots, source_row = find_frames(data_group, assignment, after_start, lengths, ROWS_G, lookup)

        def bring(array):
            picked = jnp.take(array, source_row, axis=0)
            return jnp.where(occupied_slots[:, None], picked, jnp.zeros((), array.dtype))
        context = attend(bring(query_flat), bring(key_flat), bring(value_flat), segment)
        carried = bring(residual_flat).astype(jnp.float32) + jnp.dot(context, out_proj, preferred_element_type=jnp.float32)
        average = lax.optimization_barrier(jnp.mean(carried, axis=1, keepdims=True))
        centred = carried - average
        variance = lax.optimization_barrier(jnp.mean(centred * centred, axis=1, keepdims=True))
        normed = (centred * lax.rsqrt(variance + EPS) * norm_gain + norm_bias).astype(jnp.bfloat16)
        halves = jnp.dot(normed, glu_proj, preferred_element_type=jnp.float32)
        gated_rows = (halves[:, :D] * jax.nn.sigmoid(halves[:, D:])).astype(jnp.bfloat16)
        padded = jnp.pad(gated_rows, ((HALF, HALF), (0, 0)))
        wide_segment = jnp.pad(segment, (HALF, HALF), constant_values=-2)
        convolved = depthwise(padded, wide_segment, conv_taps)
        affine = convolved * batch_scale + batch_shift
        swished = (affine * jax.nn.sigmoid(affine)).astype(jnp.bfloat16)
        lowered = jnp.dot(swished, down_proj, preferred_element_type=jnp.float32)
        return jnp.where((segment >= 0)[:, None], carried + lowered, 0.0).astype(jnp.bfloat16)
    encoded = lax.map(one_group, jnp.arange(N_DP, dtype=jnp.int32))
    return encoded.reshape(ROWS, D)
```

```python
import functools

import jax
import jax.numpy as jnp
from jax import lax
from jax.experimental import pallas as pl
from jax.experimental.pallas import tpu as pltpu
from jax.sharding import PartitionSpec as P

HD = 64
KERNEL = 31
HALF = 15
MAXLEN = 256
PIECES = 4
LANES = 128
HALO = 16
CONV_ROWS = 64

EPS = 1e-05
MASKED = -1e30
VMEM_LIMIT = 60 * 1024 * 1024


def params():
    return pltpu.CompilerParams(vmem_limit_bytes=VMEM_LIMIT)


def whole_spec():
    return pl.BlockSpec(memory_space=pltpu.VMEM)


def smem_spec():
    return pl.BlockSpec(memory_space=pltpu.SMEM)


def attention_kernel(
    heads, start_ref, span_ref, q_ref, k_ref, v_ref, out_ref, q_rows, k_rows, v_rows
):
    pairs = q_ref.shape[0]
    step = 256
    lane = lax.broadcasted_iota(jnp.int32, (step, LANES), 1)
    low = lane < HD

    def unpack(chunk, carry):
        first = pl.multiple_of(chunk * step, step)
        for packed, rows in ((q_ref, q_rows), (k_ref, k_rows), (v_ref, v_rows)):
            one = packed[pl.ds(first, step), 0:LANES].astype(jnp.float32)
            if heads == 2:
                two = packed[pl.ds(first, step), LANES : 2 * LANES].astype(jnp.float32)
                even = jnp.where(low, one, pltpu.roll(two, HD, 1))
                odd = jnp.where(low, pltpu.roll(one, HD, 1), two)
            else:
                even = one
                odd = pltpu.roll(one, HD, 1)
            rows[pl.ds(2 * first, step, stride=2), :] = even
            rows[pl.ds(2 * first + 1, step, stride=2), :] = odd
        return carry

    lax.fori_loop(0, pairs // step, unpack, 0)
    for rows in (q_rows, k_rows, v_rows):
        rows[pl.ds(2 * pairs, MAXLEN), :] = jnp.zeros((MAXLEN, LANES), jnp.float32)

    column = lax.broadcasted_iota(jnp.int32, (MAXLEN, MAXLEN), 1)
    head_lane = lax.broadcasted_iota(jnp.int32, (MAXLEN, LANES), 1) // HD

    def slot_body(slot, carry):
        start = start_ref[slot]
        allowed = column < span_ref[slot]
        queries = q_rows[pl.ds(start, MAXLEN), :]
        keys = k_rows[pl.ds(start, MAXLEN), :].astype(jnp.bfloat16)
        values = v_rows[pl.ds(start, MAXLEN), :].astype(jnp.bfloat16)
        result = None
        for head in range(heads):
            own = jnp.where(head_lane == head, queries, 0.0).astype(jnp.bfloat16)
            scores = (
                lax.dot_general(
                    own, keys, (((1,), (1,)), ((), ())), preferred_element_type=jnp.float32
                )
                * HD ** (-0.5)
            )
            scores = jnp.where(allowed, scores, MASKED)
            highest = jnp.max(scores, axis=1, keepdims=True)
            exponentials = jnp.exp(scores - highest)
            denominator = jnp.sum(exponentials, axis=1, keepdims=True)
            weights = (exponentials / denominator).astype(jnp.bfloat16)
            blended = jnp.dot(weights, values, preferred_element_type=jnp.float32)
            result = blended if head == 0 else jnp.where(head_lane == head, blended, result)
        out_ref[slot] = result[:, : heads * HD].astype(jnp.bfloat16)
        return carry

    lax.fori_loop(0, start_ref.shape[0], slot_body, 0)


def attend(start, span, query_rows, key_rows, value_rows):
    pairs, heads, _ = query_rows.shape
    slots = start.shape[0]
    flat = [a.reshape(pairs, heads * LANES) for a in (query_rows, key_rows, value_rows)]
    return pl.pallas_call(
        functools.partial(attention_kernel, heads),
        out_shape=jax.ShapeDtypeStruct((slots, MAXLEN, heads * HD), jnp.bfloat16),
        in_specs=[smem_spec()] * 2 + [whole_spec()] * 3,
        out_specs=whole_spec(),
        scratch_shapes=[pltpu.VMEM((2 * pairs + MAXLEN, LANES), jnp.float32)] * 3,
        compiler_params=params(),
        cost_estimate=pl.CostEstimate(
            flops=slots * heads * MAXLEN * MAXLEN * LANES * 4,
            bytes_accessed=pairs * heads * LANES * 8,
            transcendentals=slots * heads * MAXLEN * MAXLEN,
        ),
    )(start, span, *flat)


def lane_tiles(width):
    return [(first, min(LANES, width - first)) for first in range(0, width, LANES)]


def slots_kernel(start_ref, rows_ref, out_ref, *held):
    count, width = rows_ref.shape
    for (first, size), rows in zip(lane_tiles(width), held):

        def widen(chunk, carry):
            at = pl.multiple_of(chunk * MAXLEN, MAXLEN)
            rows[pl.ds(at, MAXLEN), 0:size] = rows_ref[
                pl.ds(at, MAXLEN), first : first + size
            ].astype(jnp.float32)
            return carry

        lax.fori_loop(0, count // MAXLEN, widen, 0)
        rows[pl.ds(count, MAXLEN), :] = jnp.zeros((MAXLEN, LANES), jnp.float32)

    def slot_body(slot, carry):
        start = start_ref[slot]
        for (first, size), rows in zip(lane_tiles(width), held):
            taken = rows[pl.ds(start, MAXLEN), :]
            out_ref[slot, :, first : first + size] = taken[:, :size].astype(jnp.bfloat16)
        return carry

    lax.fori_loop(0, start_ref.shape[0], slot_body, 0)


def into_slots(start, rows):
    count, width = rows.shape
    slots = start.shape[0]
    return pl.pallas_call(
        slots_kernel,
        out_shape=jax.ShapeDtypeStruct((slots, MAXLEN, width), jnp.bfloat16),
        in_specs=[smem_spec(), whole_spec()],
        out_specs=whole_spec(),
        scratch_shapes=[pltpu.VMEM((count + MAXLEN, LANES), jnp.float32)] * len(lane_tiles(width)),
        compiler_params=params(),
    )(start, rows)


def place_kernel(after_ref, slots_ref, out_ref, *held):
    slots, _, width = slots_ref.shape
    slabs, tall, _ = out_ref.shape
    slab_rows = tall - 2 * HALO
    total_rows = held[0].shape[0]
    zeros = jnp.zeros((MAXLEN, LANES), jnp.float32)
    for (first, size), rows in zip(lane_tiles(width), held):
        rows[pl.ds(0, HALO), :] = jnp.zeros((HALO, LANES), jnp.float32)

        def put(slot, carry):
            rows[pl.ds(HALO + after_ref[slot], MAXLEN), 0:size] = slots_ref[
                slot, :, first : first + size
            ].astype(jnp.float32)
            return carry

        lax.fori_loop(0, slots, put, 0)
        live = after_ref[slots]

        def clear(step, carry):
            at = jnp.minimum(HALO + live + step * MAXLEN, total_rows - MAXLEN)
            rows[pl.ds(at, MAXLEN), :] = zeros
            return carry

        lax.fori_loop(0, (total_rows - HALO - live + MAXLEN - 1) // MAXLEN, clear, 0)

        def emit(slab, carry):
            at = pl.multiple_of(slab * slab_rows, slab_rows)
            taken = rows[pl.ds(at, tall), :]
            out_ref[slab, :, first : first + size] = taken[:, :size].astype(jnp.bfloat16)
            return carry

        lax.fori_loop(0, slabs, emit, 0)


def place(after, slots, slabs, slab_rows):
    count, _, width = slots.shape
    return pl.pallas_call(
        place_kernel,
        out_shape=jax.ShapeDtypeStruct((slabs, slab_rows + 2 * HALO, width), jnp.bfloat16),
        in_specs=[smem_spec(), whole_spec()],
        out_specs=whole_spec(),
        scratch_shapes=[pltpu.VMEM((count * MAXLEN + HALO + MAXLEN, LANES), jnp.float32)]
        * len(lane_tiles(width)),
        compiler_params=params(),
    )(after, slots)


def conv_kernel(
    uniform_ref, gated_ref, segment_ref, taps_ref, scale_ref, shift_ref, out_ref, wide
):
    wide[...] = gated_ref[...].astype(jnp.float32)
    edge = HALO - HALF
    scale = scale_ref[...]
    shift = shift_ref[...]
    for chunk in range(out_ref.shape[0] // CONV_ROWS):
        base = chunk * CONV_ROWS

        def finish(total):
            affine = total * scale + shift
            out_ref[base : base + CONV_ROWS, :] = (affine * jax.nn.sigmoid(affine)).astype(
                jnp.bfloat16
            )

        @pl.when(uniform_ref[chunk] == 1)
        def _():
            total = jnp.zeros((CONV_ROWS, LANES), jnp.float32)
            for tap in range(KERNEL):
                total = total + wide[pl.ds(base + edge + tap, CONV_ROWS), :] * taps_ref[
                    tap : tap + 1, :
                ]
            finish(total)

        @pl.when(uniform_ref[chunk] == 0)
        def _():
            centre = segment_ref[pl.ds(base + HALO, CONV_ROWS), :]
            total = jnp.zeros((CONV_ROWS, LANES), jnp.float32)
            for tap in range(KERNEL):
                same = segment_ref[pl.ds(base + edge + tap, CONV_ROWS), :] == centre
                term = jnp.where(same, wide[pl.ds(base + edge + tap, CONV_ROWS), :], 0.0)
                total = total + term * taps_ref[tap : tap + 1, :]
            finish(total)


def convolve(gated_rows, segment, conv_taps, batch_scale, batch_shift):
    tall, width = gated_rows.shape
    rows = tall - 2 * HALO
    chunks = rows // CONV_ROWS
    windows = [segment[c * CONV_ROWS : c * CONV_ROWS + CONV_ROWS + 2 * HALO] for c in range(chunks)]
    windows = jnp.stack(windows)
    uniform = jnp.all(windows == windows[:, :1], axis=1).astype(jnp.int32)
    wide_segment = jnp.broadcast_to(segment[:, None], (tall, LANES))
    return pl.pallas_call(
        conv_kernel,
        grid=(width // LANES,),
        out_shape=jax.ShapeDtypeStruct((rows, width), jnp.bfloat16),
        in_specs=[
            smem_spec(),
            pl.BlockSpec((tall, LANES), lambda i: (0, i)),
            pl.BlockSpec((tall, LANES), lambda i: (0, 0)),
            pl.BlockSpec((KERNEL, LANES), lambda i: (0, i)),
            pl.BlockSpec((1, LANES), lambda i: (0, i)),
            pl.BlockSpec((1, LANES), lambda i: (0, i)),
        ],
        out_specs=pl.BlockSpec((rows, LANES), lambda i: (0, i)),
        scratch_shapes=[pltpu.VMEM((tall, LANES), jnp.float32)],
        compiler_params=params(),
        cost_estimate=pl.CostEstimate(
            flops=2 * rows * width * KERNEL, bytes_accessed=4 * rows * width, transcendentals=0
        ),
    )(
        uniform,
        gated_rows,
        wide_segment,
        conv_taps,
        batch_scale[None, :],
        batch_shift[None, :],
    )


def on_device(
    query_rows,
    key_rows,
    value_rows,
    residual,
    lengths,
    assignment,
    out_proj,
    norm_gain,
    norm_bias,
    glu_proj,
    conv_taps,
    batch_scale,
    batch_shift,
    down_proj,
):
    data_group = lax.axis_index("dp")
    slab_index = lax.axis_index("mp")
    groups = lax.axis_size("dp")
    slabs = lax.axis_size("mp")
    group_rows = query_rows.shape[0] * 2
    slab_rows = group_rows // slabs
    total_utterances = lengths.shape[0]
    per_group = total_utterances // groups
    slots = groups * PIECES
    features = residual.shape[2] // 4

    utterance = jnp.arange(total_utterances, dtype=jnp.int32)
    source = utterance // per_group
    earlier = utterance[None, :] < utterance[:, None]
    same_source = source[None, :] == source[:, None]
    same_target = assignment[None, :] == assignment[:, None]
    before = jnp.sum(jnp.where(earlier & same_source, lengths[None, :], 0), axis=1)
    rank = jnp.sum((earlier & same_source & same_target).astype(jnp.int32), axis=1)
    slot = jnp.arange(slots, dtype=jnp.int32)[:, None]
    leaving = (source[None, :] == data_group) & ((assignment * PIECES + rank)[None, :] == slot)
    start = jnp.sum(jnp.where(leaving, before[None, :], 0), axis=1)
    span = jnp.sum(jnp.where(leaving, lengths[None, :], 0), axis=1)
    coming = (assignment[None, :] == data_group) & ((source * PIECES + rank)[None, :] == slot)
    coming_earlier = (assignment[None, :] == data_group) & (
        (source * PIECES + rank)[None, :] < jnp.arange(slots + 1, dtype=jnp.int32)[:, None]
    )
    after = jnp.sum(jnp.where(coming_earlier, lengths[None, :], 0), axis=1)
    live = jnp.sum(jnp.where(assignment == data_group, lengths, 0))

    position = jnp.arange(slab_rows + 2 * HALO, dtype=jnp.int32) + slab_index * slab_rows - HALO
    segment = jnp.sum((position[:, None] >= after[None, 1:]).astype(jnp.int32), axis=1)
    segment = jnp.where(position < 0, -2, jnp.where(position < live, segment, -1))
    segment = jnp.where(position >= group_rows, -2, segment)

    residual_rows = (
        residual.reshape(group_rows // 4, 4, features).reshape(group_rows, features)
    )

    def swap(array, axis):
        return lax.all_to_all(array, axis, split_axis=0, concat_axis=0, tiled=True)

    def carry_over(array):
        placed = place(after, swap(array, "dp"), slabs, slab_rows)
        return swap(placed, "mp").transpose(1, 0, 2).reshape(slab_rows + 2 * HALO, -1)

    carried_slab = carry_over(into_slots(start, residual_rows))
    context_slab = carry_over(attend(start, span, query_rows, key_rows, value_rows))

    def gather(weights):
        return lax.all_gather(weights, "mp", axis=1, tiled=True)

    carried = carried_slab.astype(jnp.float32) + jnp.dot(
        context_slab, gather(out_proj), preferred_element_type=jnp.float32
    )
    average = jnp.mean(carried, axis=1, keepdims=True)
    centred = carried - average
    variance = jnp.mean(centred * centred, axis=1, keepdims=True)
    normed = (centred * lax.rsqrt(variance + EPS) * norm_gain + norm_bias).astype(jnp.bfloat16)
    halves = jnp.dot(normed, gather(glu_proj), preferred_element_type=jnp.float32)
    feature_count = halves.shape[1] // 2
    gated_rows = (halves[:, :feature_count] * jax.nn.sigmoid(halves[:, feature_count:])).astype(
        jnp.bfloat16
    )
    swished = convolve(gated_rows, segment, conv_taps, batch_scale, batch_shift)
    lowered = jnp.dot(swished, gather(down_proj), preferred_element_type=jnp.float32)
    centre_segment = segment[HALO : HALO + slab_rows]
    own_carried = carried[HALO : HALO + slab_rows]
    return jnp.where((centre_segment >= 0)[:, None], own_carried + lowered, 0.0).astype(
        jnp.bfloat16
    )


def solution(mesh):
    in_specs = (
        P("dp", "mp", None),
        P("dp", "mp", None),
        P("dp", "mp", None),
        P("dp", "mp", None),
        P(),
        P(),
        P(None, "mp"),
        P(),
        P(),
        P(None, "mp"),
        P(),
        P(),
        P(),
        P(None, "mp"),
    )
    out_specs = P(("dp", "mp"), None)
    return jax.shard_map(
        on_device, mesh=mesh, in_specs=in_specs, out_specs=out_specs, check_vma=False
    )
```

```python
import functools

import jax
import jax.numpy as jnp
from jax import lax
from jax.experimental import pallas as pl
from jax.experimental.pallas import tpu as pltpu
from jax.sharding import PartitionSpec as P

HD = 64
KERNEL = 31
HALF = 15
MAXLEN = 256
PIECES = 4
LANES = 128
HALO = 16
CONV_ROWS = 64

EPS = 1e-05
MASKED = -1e30
VMEM_LIMIT = 60 * 1024 * 1024


def params():
    return pltpu.CompilerParams(vmem_limit_bytes=VMEM_LIMIT)


def whole_spec():
    return pl.BlockSpec(memory_space=pltpu.VMEM)


def smem_spec():
    return pl.BlockSpec(memory_space=pltpu.SMEM)


def attention_kernel(
    heads, start_ref, span_ref, q_ref, k_ref, v_ref, out_ref, q_rows, k_rows, v_rows
):
    pairs = q_ref.shape[0]
    step = 256
    lane = lax.broadcasted_iota(jnp.int32, (step, LANES), 1)
    low = lane < HD

    def unpack(chunk, carry):
        first = pl.multiple_of(chunk * step, step)
        for packed, rows in ((q_ref, q_rows), (k_ref, k_rows), (v_ref, v_rows)):
            one = packed[pl.ds(first, step), 0:LANES].astype(jnp.float32)
            if heads == 2:
                two = packed[pl.ds(first, step), LANES : 2 * LANES].astype(jnp.float32)
                even = jnp.where(low, one, pltpu.roll(two, HD, 1))
                odd = jnp.where(low, pltpu.roll(one, HD, 1), two)
            else:
                even = one
                odd = pltpu.roll(one, HD, 1)
            rows[pl.ds(2 * first, step, stride=2), :] = even
            rows[pl.ds(2 * first + 1, step, stride=2), :] = odd
        return carry

    lax.fori_loop(0, pairs // step, unpack, 0)
    for rows in (q_rows, k_rows, v_rows):
        rows[pl.ds(2 * pairs, MAXLEN), :] = jnp.zeros((MAXLEN, LANES), jnp.float32)

    column = lax.broadcasted_iota(jnp.int32, (MAXLEN, MAXLEN), 1)
    head_lane = lax.broadcasted_iota(jnp.int32, (MAXLEN, LANES), 1) // HD

    def slot_body(slot, carry):
        start = start_ref[slot]
        allowed = column < span_ref[slot]
        queries = q_rows[pl.ds(start, MAXLEN), :]
        keys = k_rows[pl.ds(start, MAXLEN), :].astype(jnp.bfloat16)
        values = v_rows[pl.ds(start, MAXLEN), :].astype(jnp.bfloat16)
        result = None
        for head in range(heads):
            own = jnp.where(head_lane == head, queries, 0.0).astype(jnp.bfloat16)
            scores = (
                lax.dot_general(
                    own, keys, (((1,), (1,)), ((), ())), preferred_element_type=jnp.float32
                )
                * HD ** (-0.5)
            )
            scores = jnp.where(allowed, scores, MASKED)
            highest = jnp.max(scores, axis=1, keepdims=True)
            exponentials = jnp.exp(scores - highest)
            denominator = jnp.sum(exponentials, axis=1, keepdims=True)
            weights = (exponentials / denominator).astype(jnp.bfloat16)
            blended = jnp.dot(weights, values, preferred_element_type=jnp.float32)
            result = blended if head == 0 else jnp.where(head_lane == head, blended, result)
        out_ref[slot] = result.astype(jnp.bfloat16)
        return carry

    lax.fori_loop(0, start_ref.shape[0], slot_body, 0)


def attend(start, span, query_rows, key_rows, value_rows):
    pairs, heads, _ = query_rows.shape
    slots = start.shape[0]
    flat = [a.reshape(pairs, heads * LANES) for a in (query_rows, key_rows, value_rows)]
    return pl.pallas_call(
        functools.partial(attention_kernel, heads),
        out_shape=jax.ShapeDtypeStruct((slots, MAXLEN, LANES), jnp.bfloat16),
        in_specs=[smem_spec()] * 2 + [whole_spec()] * 3,
        out_specs=whole_spec(),
        scratch_shapes=[pltpu.VMEM((2 * pairs + MAXLEN, LANES), jnp.float32)] * 3,
        compiler_params=params(),
        cost_estimate=pl.CostEstimate(
            flops=slots * heads * MAXLEN * MAXLEN * LANES * 4,
            bytes_accessed=pairs * heads * LANES * 8,
            transcendentals=slots * heads * MAXLEN * MAXLEN,
        ),
    )(start, span, *flat)


def lane_tiles(width):
    return [(first, min(LANES, width - first)) for first in range(0, width, LANES)]


def pairable(width):
    return width == LANES + LANES // 2


def join_pair(one, two):
    half = LANES // 2
    low = lax.broadcasted_iota(jnp.int32, one[0].shape, 1) < half
    turned = pltpu.roll(two[0], half, 1)
    return (
        one[0],
        jnp.where(low, one[1], turned),
        jnp.where(low, turned, pltpu.roll(two[1], half, 1)),
    )


def split_pair(tiles):
    half = LANES // 2
    low = lax.broadcasted_iota(jnp.int32, tiles[0].shape, 1) < half
    middle = pltpu.roll(tiles[1], half, 1)
    last = pltpu.roll(tiles[2], half, 1)
    return (tiles[0], tiles[1]), (jnp.where(low, middle, last), last)


def slots_kernel(start_ref, rows_ref, out_ref, *held):
    count, width = rows_ref.shape
    for (first, size), rows in zip(lane_tiles(width), held):

        def widen(chunk, carry):
            at = pl.multiple_of(chunk * MAXLEN, MAXLEN)
            rows[pl.ds(at, MAXLEN), 0:size] = rows_ref[
                pl.ds(at, MAXLEN), first : first + size
            ].astype(jnp.float32)
            return carry

        lax.fori_loop(0, count // MAXLEN, widen, 0)
        rows[pl.ds(count, MAXLEN), :] = jnp.zeros((MAXLEN, LANES), jnp.float32)

    def slot_body(slot, carry):
        if pairable(width):
            pair = [
                [rows[pl.ds(start_ref[2 * slot + side], MAXLEN), :] for rows in held]
                for side in range(2)
            ]
            tiles = join_pair(*pair)
        else:
            tiles = [rows[pl.ds(start_ref[slot], MAXLEN), :] for rows in held]
        for index, tile in enumerate(tiles):
            out_ref[slot, :, index * LANES : (index + 1) * LANES] = tile.astype(jnp.bfloat16)
        return carry

    lax.fori_loop(0, out_ref.shape[0], slot_body, 0)


def into_slots(start, rows):
    count, width = rows.shape
    slots = start.shape[0]
    tiles = len(lane_tiles(width))
    shape = (slots, MAXLEN, tiles * LANES)
    if pairable(width):
        shape = (slots // 2, MAXLEN, 2 * width)
    return pl.pallas_call(
        slots_kernel,
        out_shape=jax.ShapeDtypeStruct(shape, jnp.bfloat16),
        in_specs=[smem_spec(), whole_spec()],
        out_specs=whole_spec(),
        scratch_shapes=[pltpu.VMEM((count + MAXLEN, LANES), jnp.float32)] * tiles,
        compiler_params=params(),
    )(start, rows)


def place_kernel(paired, after_ref, x_ref, context_ref, out_ref, context_rows, *x_rows):
    slots = context_ref.shape[0]
    slabs = out_ref.shape[0]
    tall = out_ref.shape[1] * (2 if paired else 1)
    slab_rows = tall - 2 * HALO
    total_rows = context_rows.shape[0]
    held = (context_rows,) + x_rows
    zeros = jnp.zeros((MAXLEN, LANES), jnp.float32)
    for rows in held:
        rows[pl.ds(0, HALO), :] = jnp.zeros((HALO, LANES), jnp.float32)

    def load(ref, slot, tile):
        return ref[slot, :, tile * LANES : (tile + 1) * LANES].astype(jnp.float32)

    def put(step, carry):
        if paired:
            sides = split_pair([load(x_ref, step, tile) for tile in range(3)])
            for side in range(2):
                slot = 2 * step + side
                where = pl.ds(HALO + after_ref[slot], MAXLEN)
                for rows, piece in zip(x_rows, sides[side]):
                    rows[where, :] = piece
                context_rows[where, :] = load(context_ref, slot, 0)
        else:
            where = pl.ds(HALO + after_ref[step], MAXLEN)
            for tile, rows in enumerate(x_rows):
                rows[where, :] = load(x_ref, step, tile)
            context_rows[where, :] = load(context_ref, step, 0)
        return carry

    lax.fori_loop(0, x_ref.shape[0], put, 0)
    live = after_ref[slots]

    def clear(step, carry):
        at = jnp.minimum(HALO + live + step * MAXLEN, total_rows - MAXLEN)
        for rows in held:
            rows[pl.ds(at, MAXLEN), :] = zeros
        return carry

    lax.fori_loop(0, (total_rows - HALO - live + MAXLEN - 1) // MAXLEN, clear, 0)

    def emit(slab, carry):
        at = pl.multiple_of(slab * slab_rows, slab_rows)
        if paired:
            half = tall // 2
            one = pl.ds(at, half)
            two = pl.ds(pl.multiple_of(at + half, 8), half)
            tiles = join_pair([rows[one, :] for rows in x_rows], [rows[two, :] for rows in x_rows])
            tiles = tiles + (context_rows[one, :], context_rows[two, :])
        else:
            tiles = [rows[pl.ds(at, tall), :] for rows in x_rows + (context_rows,)]
        for index, tile in enumerate(tiles):
            out_ref[slab, :, index * LANES : (index + 1) * LANES] = tile.astype(jnp.bfloat16)
        return carry

    lax.fori_loop(0, slabs, emit, 0)


def place(after, x_slots, context_slots, slabs, slab_rows, features):
    count = context_slots.shape[0]
    paired = pairable(features)
    tiles = len(lane_tiles(features))
    tall = slab_rows + 2 * HALO
    shape = (slabs, tall, (tiles + 1) * LANES)
    if paired:
        shape = (slabs, tall // 2, 2 * features + 2 * LANES)
    return pl.pallas_call(
        functools.partial(place_kernel, paired),
        out_shape=jax.ShapeDtypeStruct(shape, jnp.bfloat16),
        in_specs=[smem_spec(), whole_spec(), whole_spec()],
        out_specs=whole_spec(),
        scratch_shapes=[pltpu.VMEM((count * MAXLEN + HALO + MAXLEN, LANES), jnp.float32)]
        * (tiles + 1),
        compiler_params=params(),
    )(after, x_slots, context_slots)


def unplace(moved, features, context_width):
    slabs, rows, _ = moved.shape
    if not pairable(features):
        first = len(lane_tiles(features)) * LANES
        x = moved[:, :, :features].transpose(1, 0, 2).reshape(rows, -1)
        context = moved[:, :, first : first + context_width]
        return x, context.transpose(1, 0, 2).reshape(rows, -1)

    def sides(part, width):
        return part.reshape(slabs, rows, 2, width).transpose(2, 1, 0, 3).reshape(2 * rows, -1)

    return (
        sides(moved[:, :, : 2 * features], features),
        sides(moved[:, :, 2 * features :], context_width),
    )


def conv_kernel(
    uniform_ref, gated_ref, segment_ref, taps_ref, scale_ref, shift_ref, out_ref, wide
):
    wide[...] = gated_ref[...].astype(jnp.float32)
    edge = HALO - HALF
    scale = scale_ref[...]
    shift = shift_ref[...]
    for chunk in range(out_ref.shape[0] // CONV_ROWS):
        base = chunk * CONV_ROWS

        def finish(total):
            affine = total * scale + shift
            out_ref[base : base + CONV_ROWS, :] = (affine * jax.nn.sigmoid(affine)).astype(
                jnp.bfloat16
            )

        @pl.when(uniform_ref[chunk] == 1)
        def _():
            total = jnp.zeros((CONV_ROWS, LANES), jnp.float32)
            for tap in range(KERNEL):
                total = total + wide[pl.ds(base + edge + tap, CONV_ROWS), :] * taps_ref[
                    tap : tap + 1, :
                ]
            finish(total)

        @pl.when(uniform_ref[chunk] == 0)
        def _():
            centre = segment_ref[pl.ds(base + HALO, CONV_ROWS), :]
            total = jnp.zeros((CONV_ROWS, LANES), jnp.float32)
            for tap in range(KERNEL):
                same = segment_ref[pl.ds(base + edge + tap, CONV_ROWS), :] == centre
                term = jnp.where(same, wide[pl.ds(base + edge + tap, CONV_ROWS), :], 0.0)
                total = total + term * taps_ref[tap : tap + 1, :]
            finish(total)


def convolve(gated_rows, segment, conv_taps, batch_scale, batch_shift):
    tall, width = gated_rows.shape
    rows = tall - 2 * HALO
    chunks = rows // CONV_ROWS
    windows = [segment[c * CONV_ROWS : c * CONV_ROWS + CONV_ROWS + 2 * HALO] for c in range(chunks)]
    windows = jnp.stack(windows)
    uniform = jnp.all(windows == windows[:, :1], axis=1).astype(jnp.int32)
    wide_segment = jnp.broadcast_to(segment[:, None], (tall, LANES))
    return pl.pallas_call(
        conv_kernel,
        grid=(width // LANES,),
        out_shape=jax.ShapeDtypeStruct((rows, width), jnp.bfloat16),
        in_specs=[
            smem_spec(),
            pl.BlockSpec((tall, LANES), lambda i: (0, i)),
            pl.BlockSpec((tall, LANES), lambda i: (0, 0)),
            pl.BlockSpec((KERNEL, LANES), lambda i: (0, i)),
            pl.BlockSpec((1, LANES), lambda i: (0, i)),
            pl.BlockSpec((1, LANES), lambda i: (0, i)),
        ],
        out_specs=pl.BlockSpec((rows, LANES), lambda i: (0, i)),
        scratch_shapes=[pltpu.VMEM((tall, LANES), jnp.float32)],
        compiler_params=params(),
        cost_estimate=pl.CostEstimate(
            flops=2 * rows * width * KERNEL, bytes_accessed=4 * rows * width, transcendentals=0
        ),
    )(
        uniform,
        gated_rows,
        wide_segment,
        conv_taps,
        batch_scale[None, :],
        batch_shift[None, :],
    )


def on_device(
    query_rows,
    key_rows,
    value_rows,
    residual,
    lengths,
    assignment,
    out_proj,
    norm_gain,
    norm_bias,
    glu_proj,
    conv_taps,
    batch_scale,
    batch_shift,
    down_proj,
):
    data_group = lax.axis_index("dp")
    slab_index = lax.axis_index("mp")
    groups = lax.axis_size("dp")
    slabs = lax.axis_size("mp")
    group_rows = query_rows.shape[0] * 2
    slab_rows = group_rows // slabs
    total_utterances = lengths.shape[0]
    per_group = total_utterances // groups
    slots = groups * PIECES
    features = residual.shape[2] // 4

    utterance = jnp.arange(total_utterances, dtype=jnp.int32)
    source = utterance // per_group
    earlier = utterance[None, :] < utterance[:, None]
    same_source = source[None, :] == source[:, None]
    same_target = assignment[None, :] == assignment[:, None]
    before = jnp.sum(jnp.where(earlier & same_source, lengths[None, :], 0), axis=1)
    rank = jnp.sum((earlier & same_source & same_target).astype(jnp.int32), axis=1)
    slot = jnp.arange(slots, dtype=jnp.int32)[:, None]
    leaving = (source[None, :] == data_group) & ((assignment * PIECES + rank)[None, :] == slot)
    start = jnp.sum(jnp.where(leaving, before[None, :], 0), axis=1)
    span = jnp.sum(jnp.where(leaving, lengths[None, :], 0), axis=1)
    coming_earlier = (assignment[None, :] == data_group) & (
        (source * PIECES + rank)[None, :] < jnp.arange(slots + 1, dtype=jnp.int32)[:, None]
    )
    after = jnp.sum(jnp.where(coming_earlier, lengths[None, :], 0), axis=1)
    live = jnp.sum(jnp.where(assignment == data_group, lengths, 0))

    position = jnp.arange(slab_rows + 2 * HALO, dtype=jnp.int32) + slab_index * slab_rows - HALO
    segment = jnp.sum((position[:, None] >= after[None, 1:]).astype(jnp.int32), axis=1)
    segment = jnp.where(position < 0, -2, jnp.where(position < live, segment, -1))
    segment = jnp.where(position >= group_rows, -2, segment)

    residual_rows = (
        residual.reshape(group_rows // 4, 4, features).reshape(group_rows, features)
    )

    def swap(array, axis):
        return lax.all_to_all(array, axis, split_axis=0, concat_axis=0, tiled=True)

    x_slots = swap(into_slots(start, residual_rows), "dp")
    context_slots = swap(attend(start, span, query_rows, key_rows, value_rows), "dp")
    moved = swap(place(after, x_slots, context_slots, slabs, slab_rows, features), "mp")
    carried_slab, context_slab = unplace(moved, features, query_rows.shape[1] * HD)

    core = data_group % 2
    partners = [(group, group + 1 - 2 * (group % 2)) for group in range(groups)]

    def gather(weights):
        half = weights.shape[0] // 2
        own = lax.dynamic_slice_in_dim(weights, core * half, half, 0)
        own = lax.all_gather(own, "mp", axis=1, tiled=True)
        return own, lax.ppermute(own, "dp", partners)

    def project(rows, halves_of):
        own, other = halves_of
        half = rows.shape[1] // 2
        low, high = rows[:, :half], rows[:, half:]
        return jnp.dot(
            jnp.where(core == 0, low, high), own, preferred_element_type=jnp.float32
        ) + jnp.dot(jnp.where(core == 0, high, low), other, preferred_element_type=jnp.float32)

    out_halves, glu_halves, down_halves = gather(out_proj), gather(glu_proj), gather(down_proj)
    carried = carried_slab.astype(jnp.float32) + project(context_slab, out_halves)
    average = jnp.mean(carried, axis=1, keepdims=True)
    centred = carried - average
    variance = jnp.mean(centred * centred, axis=1, keepdims=True)
    normed = (centred * lax.rsqrt(variance + EPS) * norm_gain + norm_bias).astype(jnp.bfloat16)
    halves = project(normed, glu_halves)
    feature_count = halves.shape[1] // 2
    gated_rows = (halves[:, :feature_count] * jax.nn.sigmoid(halves[:, feature_count:])).astype(
        jnp.bfloat16
    )
    swished = convolve(gated_rows, segment, conv_taps, batch_scale, batch_shift)
    lowered = project(swished, down_halves)
    centre_segment = segment[HALO : HALO + slab_rows]
    own_carried = carried[HALO : HALO + slab_rows]
    return jnp.where((centre_segment >= 0)[:, None], own_carried + lowered, 0.0).astype(
        jnp.bfloat16
    )


def solution(mesh):
    in_specs = (
        P("dp", "mp", None),
        P("dp", "mp", None),
        P("dp", "mp", None),
        P("dp", "mp", None),
        P(),
        P(),
        P(None, "mp"),
        P(),
        P(),
        P(None, "mp"),
        P(),
        P(),
        P(),
        P(None, "mp"),
    )
    out_specs = P(("dp", "mp"), None)
    return jax.shard_map(
        on_device, mesh=mesh, in_specs=in_specs, out_specs=out_specs, check_vma=False
    )
```

```python
import functools

import jax
import jax.numpy as jnp
from jax import lax
from jax.experimental import pallas as pl
from jax.experimental.pallas import tpu as pltpu
from jax.sharding import PartitionSpec as P

HD = 64
KERNEL = 31
HALF = 15
MAXLEN = 256
PIECES = 4
LANES = 128
HALO = 16
CONV_ROWS = 64

EPS = 1e-05
MASKED = -1e30
VMEM_LIMIT = 60 * 1024 * 1024


def params():
    return pltpu.CompilerParams(vmem_limit_bytes=VMEM_LIMIT)


def whole_spec():
    return pl.BlockSpec(memory_space=pltpu.VMEM)


def smem_spec():
    return pl.BlockSpec(memory_space=pltpu.SMEM)


def attention_kernel(
    heads, start_ref, span_ref, q_ref, k_ref, v_ref, out_ref, q_rows, k_rows, v_rows
):
    pairs = q_ref.shape[0]
    step = 256
    lane = lax.broadcasted_iota(jnp.int32, (step, LANES), 1)
    low = lane < HD

    def unpack(chunk, carry):
        first = pl.multiple_of(chunk * step, step)
        for packed, rows in ((q_ref, q_rows), (k_ref, k_rows), (v_ref, v_rows)):
            one = packed[pl.ds(first, step), 0:LANES].astype(jnp.float32)
            if heads == 2:
                two = packed[pl.ds(first, step), LANES : 2 * LANES].astype(jnp.float32)
                even = jnp.where(low, one, pltpu.roll(two, HD, 1))
                odd = jnp.where(low, pltpu.roll(one, HD, 1), two)
            else:
                even = one
                odd = pltpu.roll(one, HD, 1)
            rows[pl.ds(2 * first, step, stride=2), :] = even
            rows[pl.ds(2 * first + 1, step, stride=2), :] = odd
        return carry

    lax.fori_loop(0, pairs // step, unpack, 0)
    for rows in (q_rows, k_rows, v_rows):
        rows[pl.ds(2 * pairs, MAXLEN), :] = jnp.zeros((MAXLEN, LANES), jnp.float32)

    column = lax.broadcasted_iota(jnp.int32, (MAXLEN, MAXLEN), 1)
    head_lane = lax.broadcasted_iota(jnp.int32, (MAXLEN, LANES), 1) // HD

    def slot_body(slot, carry):
        start = start_ref[slot]
        allowed = column < span_ref[slot]
        queries = q_rows[pl.ds(start, MAXLEN), :]
        keys = k_rows[pl.ds(start, MAXLEN), :].astype(jnp.bfloat16)
        values = v_rows[pl.ds(start, MAXLEN), :].astype(jnp.bfloat16)
        result = None
        for head in range(heads):
            own = jnp.where(head_lane == head, queries, 0.0).astype(jnp.bfloat16)
            scores = (
                lax.dot_general(
                    own, keys, (((1,), (1,)), ((), ())), preferred_element_type=jnp.float32
                )
                * HD ** (-0.5)
            )
            scores = jnp.where(allowed, scores, MASKED)
            highest = jnp.max(scores, axis=1, keepdims=True)
            exponentials = jnp.exp(scores - highest)
            denominator = jnp.sum(exponentials, axis=1, keepdims=True)
            weights = (exponentials / denominator).astype(jnp.bfloat16)
            blended = jnp.dot(weights, values, preferred_element_type=jnp.float32)
            result = blended if head == 0 else jnp.where(head_lane == head, blended, result)
        out_ref[slot] = result.astype(jnp.bfloat16)
        return carry

    lax.fori_loop(0, start_ref.shape[0], slot_body, 0)


def attend(start, span, query_rows, key_rows, value_rows):
    pairs, heads, _ = query_rows.shape
    slots = start.shape[0]
    flat = [a.reshape(pairs, heads * LANES) for a in (query_rows, key_rows, value_rows)]
    return pl.pallas_call(
        functools.partial(attention_kernel, heads),
        out_shape=jax.ShapeDtypeStruct((slots, MAXLEN, LANES), jnp.bfloat16),
        in_specs=[smem_spec()] * 2 + [whole_spec()] * 3,
        out_specs=whole_spec(),
        scratch_shapes=[pltpu.VMEM((2 * pairs + MAXLEN, LANES), jnp.float32)] * 3,
        compiler_params=params(),
        cost_estimate=pl.CostEstimate(
            flops=slots * heads * MAXLEN * MAXLEN * LANES * 4,
            bytes_accessed=pairs * heads * LANES * 8,
            transcendentals=slots * heads * MAXLEN * MAXLEN,
        ),
    )(start, span, *flat)


def lane_tiles(width):
    return [(first, min(LANES, width - first)) for first in range(0, width, LANES)]


def pairable(width):
    return width == LANES + LANES // 2


def join_pair(one, two):
    half = LANES // 2
    low = lax.broadcasted_iota(jnp.int32, one[0].shape, 1) < half
    turned = pltpu.roll(two[0], half, 1)
    return (
        one[0],
        jnp.where(low, one[1], turned),
        jnp.where(low, turned, pltpu.roll(two[1], half, 1)),
    )


def split_pair(tiles):
    half = LANES // 2
    low = lax.broadcasted_iota(jnp.int32, tiles[0].shape, 1) < half
    middle = pltpu.roll(tiles[1], half, 1)
    last = pltpu.roll(tiles[2], half, 1)
    return (tiles[0], tiles[1]), (jnp.where(low, middle, last), last)


def slots_kernel(start_ref, rows_ref, out_ref, *held):
    count, width = rows_ref.shape
    for (first, size), rows in zip(lane_tiles(width), held):

        def widen(chunk, carry):
            at = pl.multiple_of(chunk * MAXLEN, MAXLEN)
            rows[pl.ds(at, MAXLEN), 0:size] = rows_ref[
                pl.ds(at, MAXLEN), first : first + size
            ].astype(jnp.float32)
            return carry

        lax.fori_loop(0, count // MAXLEN, widen, 0)
        rows[pl.ds(count, MAXLEN), :] = jnp.zeros((MAXLEN, LANES), jnp.float32)

    def slot_body(slot, carry):
        if pairable(width):
            pair = [
                [rows[pl.ds(start_ref[2 * slot + side], MAXLEN), :] for rows in held]
                for side in range(2)
            ]
            tiles = join_pair(*pair)
        else:
            tiles = [rows[pl.ds(start_ref[slot], MAXLEN), :] for rows in held]
        for index, tile in enumerate(tiles):
            out_ref[slot, :, index * LANES : (index + 1) * LANES] = tile.astype(jnp.bfloat16)
        return carry

    lax.fori_loop(0, out_ref.shape[0], slot_body, 0)


def into_slots(start, rows):
    count, width = rows.shape
    slots = start.shape[0]
    tiles = len(lane_tiles(width))
    shape = (slots, MAXLEN, tiles * LANES)
    if pairable(width):
        shape = (slots // 2, MAXLEN, 2 * width)
    return pl.pallas_call(
        slots_kernel,
        out_shape=jax.ShapeDtypeStruct(shape, jnp.bfloat16),
        in_specs=[smem_spec(), whole_spec()],
        out_specs=whole_spec(),
        scratch_shapes=[pltpu.VMEM((count + MAXLEN, LANES), jnp.float32)] * tiles,
        compiler_params=params(),
    )(start, rows)


def place_kernel(paired, after_ref, x_ref, context_ref, out_ref, context_rows, *x_rows):
    slots = context_ref.shape[0]
    slabs = out_ref.shape[0]
    tall = out_ref.shape[1] * (2 if paired else 1)
    slab_rows = tall - 2 * HALO
    total_rows = context_rows.shape[0]
    held = (context_rows,) + x_rows
    zeros = jnp.zeros((MAXLEN, LANES), jnp.float32)
    for rows in held:
        rows[pl.ds(0, HALO), :] = jnp.zeros((HALO, LANES), jnp.float32)

    def load(ref, slot, tile):
        return ref[slot, :, tile * LANES : (tile + 1) * LANES].astype(jnp.float32)

    def put(step, carry):
        if paired:
            sides = split_pair([load(x_ref, step, tile) for tile in range(3)])
            for side in range(2):
                slot = 2 * step + side
                where = pl.ds(HALO + after_ref[slot], MAXLEN)
                for rows, piece in zip(x_rows, sides[side]):
                    rows[where, :] = piece
                context_rows[where, :] = load(context_ref, slot, 0)
        else:
            where = pl.ds(HALO + after_ref[step], MAXLEN)
            for tile, rows in enumerate(x_rows):
                rows[where, :] = load(x_ref, step, tile)
            context_rows[where, :] = load(context_ref, step, 0)
        return carry

    lax.fori_loop(0, x_ref.shape[0], put, 0)
    live = after_ref[slots]

    def clear(step, carry):
        at = jnp.minimum(HALO + live + step * MAXLEN, total_rows - MAXLEN)
        for rows in held:
            rows[pl.ds(at, MAXLEN), :] = zeros
        return carry

    lax.fori_loop(0, (total_rows - HALO - live + MAXLEN - 1) // MAXLEN, clear, 0)

    def emit(slab, carry):
        at = pl.multiple_of(slab * slab_rows, slab_rows)
        if paired:
            half = tall // 2
            one = pl.ds(at, half)
            two = pl.ds(pl.multiple_of(at + half, 8), half)
            tiles = join_pair([rows[one, :] for rows in x_rows], [rows[two, :] for rows in x_rows])
            tiles = tiles + (context_rows[one, :], context_rows[two, :])
        else:
            tiles = [rows[pl.ds(at, tall), :] for rows in x_rows + (context_rows,)]
        for index, tile in enumerate(tiles):
            out_ref[slab, :, index * LANES : (index + 1) * LANES] = tile.astype(jnp.bfloat16)
        return carry

    lax.fori_loop(0, slabs, emit, 0)


def place(after, x_slots, context_slots, slabs, slab_rows, features):
    count = context_slots.shape[0]
    paired = pairable(features)
    tiles = len(lane_tiles(features))
    tall = slab_rows + 2 * HALO
    shape = (slabs, tall, (tiles + 1) * LANES)
    if paired:
        shape = (slabs, tall // 2, 2 * features + 2 * LANES)
    return pl.pallas_call(
        functools.partial(place_kernel, paired),
        out_shape=jax.ShapeDtypeStruct(shape, jnp.bfloat16),
        in_specs=[smem_spec(), whole_spec(), whole_spec()],
        out_specs=whole_spec(),
        scratch_shapes=[pltpu.VMEM((count * MAXLEN + HALO + MAXLEN, LANES), jnp.float32)]
        * (tiles + 1),
        compiler_params=params(),
    )(after, x_slots, context_slots)


def unplace_kernel(moved_ref, x_ref, context_ref):
    slabs, rows, _ = moved_ref.shape
    step = 16
    span = 3 * LANES

    def chunk(index, carry):
        at = pl.multiple_of(index * step, step)

        def load(slab, tile):
            cells = moved_ref[slab, pl.ds(at, step), tile * LANES : (tile + 1) * LANES]
            return cells.astype(jnp.float32)

        for pair in range(slabs // 2):
            split = [
                split_pair([load(2 * pair + member, tile) for tile in range(3)])
                for member in range(2)
            ]
            for side in range(2):
                to = pl.ds(pl.multiple_of(at + side * rows, step), step)
                for tile, cells in enumerate(join_pair(split[0][side], split[1][side])):
                    first = pair * span + tile * LANES
                    x_ref[to, first : first + LANES] = cells.astype(jnp.bfloat16)
        for slab in range(slabs):
            for side in range(2):
                to = pl.ds(pl.multiple_of(at + side * rows, step), step)
                first = span + side * LANES
                context_ref[to, slab * LANES : (slab + 1) * LANES] = moved_ref[
                    slab, pl.ds(at, step), first : first + LANES
                ]
        return carry

    lax.fori_loop(0, rows // step, chunk, 0)


def unplace(moved, features, context_width):
    slabs, rows, _ = moved.shape
    if not (pairable(features) and context_width == LANES):
        first = len(lane_tiles(features)) * LANES
        x = moved[:, :, :features].transpose(1, 0, 2).reshape(rows, -1)
        context = moved[:, :, first : first + context_width]
        return x, context.transpose(1, 0, 2).reshape(rows, -1)
    return pl.pallas_call(
        unplace_kernel,
        out_shape=(
            jax.ShapeDtypeStruct((2 * rows, slabs * features), jnp.bfloat16),
            jax.ShapeDtypeStruct((2 * rows, slabs * context_width), jnp.bfloat16),
        ),
        in_specs=[whole_spec()],
        out_specs=(whole_spec(), whole_spec()),
        compiler_params=params(),
    )(moved)


def conv_kernel(
    uniform_ref, gated_ref, segment_ref, taps_ref, scale_ref, shift_ref, out_ref, wide
):
    wide[...] = gated_ref[...].astype(jnp.float32)
    edge = HALO - HALF
    scale = scale_ref[...]
    shift = shift_ref[...]
    for chunk in range(out_ref.shape[0] // CONV_ROWS):
        base = chunk * CONV_ROWS

        def finish(total):
            affine = total * scale + shift
            out_ref[base : base + CONV_ROWS, :] = (affine * jax.nn.sigmoid(affine)).astype(
                jnp.bfloat16
            )

        @pl.when(uniform_ref[chunk] == 1)
        def _():
            total = jnp.zeros((CONV_ROWS, LANES), jnp.float32)
            for tap in range(KERNEL):
                total = total + wide[pl.ds(base + edge + tap, CONV_ROWS), :] * taps_ref[
                    tap : tap + 1, :
                ]
            finish(total)

        @pl.when(uniform_ref[chunk] == 0)
        def _():
            centre = segment_ref[pl.ds(base + HALO, CONV_ROWS), :]
            total = jnp.zeros((CONV_ROWS, LANES), jnp.float32)
            for tap in range(KERNEL):
                same = segment_ref[pl.ds(base + edge + tap, CONV_ROWS), :] == centre
                term = jnp.where(same, wide[pl.ds(base + edge + tap, CONV_ROWS), :], 0.0)
                total = total + term * taps_ref[tap : tap + 1, :]
            finish(total)


def convolve(gated_rows, segment, conv_taps, batch_scale, batch_shift):
    tall, width = gated_rows.shape
    rows = tall - 2 * HALO
    chunks = rows // CONV_ROWS
    windows = [segment[c * CONV_ROWS : c * CONV_ROWS + CONV_ROWS + 2 * HALO] for c in range(chunks)]
    windows = jnp.stack(windows)
    uniform = jnp.all(windows == windows[:, :1], axis=1).astype(jnp.int32)
    wide_segment = jnp.broadcast_to(segment[:, None], (tall, LANES))
    return pl.pallas_call(
        conv_kernel,
        grid=(width // LANES,),
        out_shape=jax.ShapeDtypeStruct((rows, width), jnp.bfloat16),
        in_specs=[
            smem_spec(),
            pl.BlockSpec((tall, LANES), lambda i: (0, i)),
            pl.BlockSpec((tall, LANES), lambda i: (0, 0)),
            pl.BlockSpec((KERNEL, LANES), lambda i: (0, i)),
            pl.BlockSpec((1, LANES), lambda i: (0, i)),
            pl.BlockSpec((1, LANES), lambda i: (0, i)),
        ],
        out_specs=pl.BlockSpec((rows, LANES), lambda i: (0, i)),
        scratch_shapes=[pltpu.VMEM((tall, LANES), jnp.float32)],
        compiler_params=params(),
        cost_estimate=pl.CostEstimate(
            flops=2 * rows * width * KERNEL, bytes_accessed=4 * rows * width, transcendentals=0
        ),
    )(
        uniform,
        gated_rows,
        wide_segment,
        conv_taps,
        batch_scale[None, :],
        batch_shift[None, :],
    )


def on_device(
    query_rows,
    key_rows,
    value_rows,
    residual,
    lengths,
    assignment,
    out_proj,
    norm_gain,
    norm_bias,
    glu_proj,
    conv_taps,
    batch_scale,
    batch_shift,
    down_proj,
):
    data_group = lax.axis_index("dp")
    slab_index = lax.axis_index("mp")
    groups = lax.axis_size("dp")
    slabs = lax.axis_size("mp")
    group_rows = query_rows.shape[0] * 2
    slab_rows = group_rows // slabs
    total_utterances = lengths.shape[0]
    per_group = total_utterances // groups
    slots = groups * PIECES
    features = residual.shape[2] // 4

    utterance = jnp.arange(total_utterances, dtype=jnp.int32)
    source = utterance // per_group
    earlier = utterance[None, :] < utterance[:, None]
    same_source = source[None, :] == source[:, None]
    same_target = assignment[None, :] == assignment[:, None]
    before = jnp.sum(jnp.where(earlier & same_source, lengths[None, :], 0), axis=1)
    rank = jnp.sum((earlier & same_source & same_target).astype(jnp.int32), axis=1)
    slot = jnp.arange(slots, dtype=jnp.int32)[:, None]
    leaving = (source[None, :] == data_group) & ((assignment * PIECES + rank)[None, :] == slot)
    start = jnp.sum(jnp.where(leaving, before[None, :], 0), axis=1)
    span = jnp.sum(jnp.where(leaving, lengths[None, :], 0), axis=1)
    coming_earlier = (assignment[None, :] == data_group) & (
        (source * PIECES + rank)[None, :] < jnp.arange(slots + 1, dtype=jnp.int32)[:, None]
    )
    after = jnp.sum(jnp.where(coming_earlier, lengths[None, :], 0), axis=1)
    live = jnp.sum(jnp.where(assignment == data_group, lengths, 0))

    position = jnp.arange(slab_rows + 2 * HALO, dtype=jnp.int32) + slab_index * slab_rows - HALO
    segment = jnp.sum((position[:, None] >= after[None, 1:]).astype(jnp.int32), axis=1)
    segment = jnp.where(position < 0, -2, jnp.where(position < live, segment, -1))
    segment = jnp.where(position >= group_rows, -2, segment)

    residual_rows = (
        residual.reshape(group_rows // 4, 4, features).reshape(group_rows, features)
    )

    def swap(array, axis):
        return lax.all_to_all(array, axis, split_axis=0, concat_axis=0, tiled=True)

    packed, start = lax.optimization_barrier((into_slots(start, residual_rows), start))
    x_slots = swap(packed, "dp")
    context_slots = swap(attend(start, span, query_rows, key_rows, value_rows), "dp")
    moved = swap(place(after, x_slots, context_slots, slabs, slab_rows, features), "mp")
    carried_slab, context_slab = unplace(moved, features, query_rows.shape[1] * HD)

    core = data_group % 2
    partners = [(group, group + 1 - 2 * (group % 2)) for group in range(groups)]

    def gather(weights):
        half = weights.shape[0] // 2
        own = lax.dynamic_slice_in_dim(weights, core * half, half, 0)
        return lax.all_gather(own, "mp", axis=1, tiled=True)

    def both(own):
        return own, lax.ppermute(own, "dp", partners)

    def project(rows, halves_of):
        own, other = halves_of
        half = rows.shape[1] // 2
        low, high = rows[:, :half], rows[:, half:]
        return jnp.dot(
            jnp.where(core == 0, low, high), own, preferred_element_type=jnp.float32
        ) + jnp.dot(jnp.where(core == 0, high, low), other, preferred_element_type=jnp.float32)

    out_halves, glu_halves = both(gather(out_proj)), both(gather(glu_proj))
    down_own = gather(down_proj)
    carried = carried_slab.astype(jnp.float32) + project(context_slab, out_halves)
    average = jnp.mean(carried, axis=1, keepdims=True)
    centred = carried - average
    variance = jnp.mean(centred * centred, axis=1, keepdims=True)
    normed = (centred * lax.rsqrt(variance + EPS) * norm_gain + norm_bias).astype(jnp.bfloat16)
    halves = project(normed, glu_halves)
    feature_count = halves.shape[1] // 2
    gated_rows = (halves[:, :feature_count] * jax.nn.sigmoid(halves[:, feature_count:])).astype(
        jnp.bfloat16
    )
    down_own, gated_rows = lax.optimization_barrier((down_own, gated_rows))
    down_halves = both(down_own)
    swished = convolve(gated_rows, segment, conv_taps, batch_scale, batch_shift)
    lowered = project(swished, down_halves)
    centre_segment = segment[HALO : HALO + slab_rows]
    own_carried = carried[HALO : HALO + slab_rows]
    return jnp.where((centre_segment >= 0)[:, None], own_carried + lowered, 0.0).astype(
        jnp.bfloat16
    )


def solution(mesh):
    in_specs = (
        P("dp", "mp", None),
        P("dp", "mp", None),
        P("dp", "mp", None),
        P("dp", "mp", None),
        P(),
        P(),
        P(None, "mp"),
        P(),
        P(),
        P(None, "mp"),
        P(),
        P(),
        P(),
        P(None, "mp"),
    )
    out_specs = P(("dp", "mp"), None)
    return jax.shard_map(
        on_device, mesh=mesh, in_specs=in_specs, out_specs=out_specs, check_vma=False
    )
```
